32 devices in a mesh: gx: 8 (over z, y), pb: 4 (over x, core).
Axes of the slice: x: 2, y: 2, z: 4, core: 2. Of those that a mesh axis runs over, the one named last changes fastest.
Arguments:
- density: float32 [16, 128, 128], P('gx', 'pb'), may hold values from 0.5 to 2
- velocity: float32 [3, 16, 128, 128], P(None, 'gx', 'pb'), may hold values from -3 to 3
- magnetic: float32 [3, 16, 128, 128], P(None, 'gx', 'pb'), may hold values from -4 to 4
- pressure: float32 [16, 128, 128], P('gx', 'pb'), may hold values from 0.2 to 2
- line_owner: int32 [8, 4, 64, 1], P('gx', 'pb'), may hold values from 0 to 7; in each aligned block of 64 rows (0 to 63, 64 to 127, ..., all dimensions but the last counted through in order) at most 16 rows name the same one
- line_row: int32 [8, 4, 64], P('gx', 'pb'), may hold values from 0 to 7
- pedersen: float32 [256, 128], P(('gx', 'pb')), may hold values from 0.5 to 8
- hall: float32 [256, 128], P(('gx', 'pb')), may hold values from 0.3 to 5
- mirror_shift: int32 [256], P(('gx', 'pb')), may hold values from 0 to 127, as said below
Outputs:
- conserved: float32 [8, 16, 128, 128], P(None, 'gx', 'pb')
- potential: float32 [256, 128], P(('gx', 'pb'))
The draws below stay inside these ranges and needn't reach their ends.
Inputs may be any that keep to these rules, and one draw needn't show every extreme that they name: `line_owner`: among the rows of one device no owner index is named more than 16 times. `mirror_shift`: entry r + 128 equals (128 - entry r) mod 128 for every row r below 128.
All inputs are finite; a program needn't handle non-finite values.
Results may differ from the reference program's by a relative error of at most 0.0003.
Values sent between devices are 32-bit elements; how exact they have to be, the bound alone decides.
A program may use at most 64 MiB of HBM per device.

```python
import math
import jax
import jax.numpy as jnp
import numpy as np
from jax import lax

CX = 2
CY = 32
NZ = 128
RI = 8
SWEEPS = 8
NX = 16
NY = 128
ROWS_DEV = 64
CAP = 16
NLAT = 256
ILAT = 128
ILON = 128
N_GX = 8
N_PB = 4


def draw_mirror_shift(key, part):
    northern = jax.random.randint(key, (ILAT,), 0, ILON, dtype=jnp.int32)
    southern = (ILON - northern) % ILON
    return jnp.concatenate([northern, southern])


def with_ends(values, own_key, low, top_value):
    extent = values.shape
    place = [jax.random.randint(jax.random.fold_in(own_key, axis), (), 0, extent[axis]) for axis in range(len(extent))]
    values = values.at[tuple(place)].set(low)
    longest = extent.index(max(extent))
    place[longest] = (place[longest] + 1) % extent[longest]
    return values.at[tuple(place)].set(top_value)


def levels(stream_key, dims, shards, least, high):
    factor_of = 1.0
    for axis_at, shards_of in shards:
        heights = jax.random.uniform(jax.random.fold_in(jax.random.fold_in(stream_key, 6), axis_at), (shards_of,), jnp.float32, least / len(shards), high / len(shards))
        factor_of = factor_of * jnp.repeat(jnp.exp(heights), dims[axis_at] // shards_of).reshape((-1,) + (1,) * (len(dims) - 1 - axis_at))
    return factor_of


def routed_block(key, own, number, rows, count, top, limit, slope):
    ranking = jax.random.permutation(key, count)
    heavy_load, usual = load_shares(count, rows * top, limit, slope, True), load_shares(count, rows * top, limit, slope, False)
    places = jnp.arange(count)

    def named(sizes, turn):
        used = int((sizes > 0).sum())
        fixed = max(1, used // 4)
        shifted = fixed + (places - fixed + turn * (used - fixed)) % max(1, count - fixed)
        return jnp.zeros((count,), jnp.int32).at[ranking[jnp.where(places < fixed, places, shifted)]].set(jnp.asarray(sizes, jnp.int32))

    sizes = jnp.where(number % 4 == 0, named(heavy_load, number // 4), named(usual, number - number // 4 - 1))
    mixed = jax.random.permutation(jax.random.fold_in(own, 3), count)
    donor, sink = mixed[0:count // 2 * 2:2], mixed[1:count // 2 * 2:2]
    room = jnp.minimum(sizes[donor] - 1, limit - sizes[sink]) // 2
    room = jnp.where((donor == ranking[0]) | (sink == ranking[0]) | (sizes[sink] == 0), 0, jnp.maximum(room, 0))
    shifted = jax.random.randint(jax.random.fold_in(own, 4), (count // 2,), 0, 1 << 20) % (room + 1)
    sizes = sizes.at[donor].add(-shifted).at[sink].add(shifted)
    members = jnp.searchsorted(jnp.cumsum(sizes), jnp.arange(rows * top), side="right").astype(jnp.int32)
    table = members.reshape(top, rows).T
    table = table[jax.random.permutation(jax.random.fold_in(own, 1), rows)]
    turn = jax.random.randint(jax.random.fold_in(own, 2), (rows, 1), 0, top)
    return jnp.take_along_axis(table, (jnp.arange(top)[None, :] + turn) % top, axis=1)


def load_shares(count, total, limit, lean, full):
    weights = [(1 << 20) // math.isqrt(standing ** lean) + 1 for standing in range(1, count + 1)]
    largest = limit if full else min(limit, max(-(-total // count), total * weights[0] // sum(weights)))
    least = 1 if total - largest >= count - 1 else 0
    holding, surplus = [largest] + [least] * (count - 1), total - largest - least * (count - 1)
    while surplus > 0:
        movable = [i for i in range(1, count) if holding[i] < largest] or [i for i in range(1, count) if holding[i] < limit]
        mass, left = sum([weights[i] for i in movable]), surplus
        for i in movable:
            addition = min(limit - holding[i], max(1, left * weights[i] // mass), surplus)
            holding[i] = holding[i] + addition
            surplus = surplus - addition
    return np.array(holding)


def noise(key, extent, width, most, cuts=(), kind=jnp.bfloat16):
    array = jax.random.normal(key, extent, jnp.float32) * width
    if len(cuts) > 0:
        array = levels(key, extent, cuts, -0.22, 0.18) * array
    return jnp.clip(array, min=-most, max=most).astype(kind)


def setup_inputs(seed: int = 0) -> dict:
    key_list = jax.random.split(jax.random.key(seed), 10)
    density = jnp.clip(0.5 + 1.5 * jax.random.uniform(key_list[0], (NX, NY, NZ), jnp.float32) ** levels(key_list[0], (NX, NY, NZ), ((0, 8), (1, 4)), -0.2, 0.2), 0.5, 2.0)
    velocity = noise(key_list[1], (3, NX, NY, NZ), 0.5, 3.0, ((1, 8), (2, 4)), jnp.float32)
    magnetic = noise(key_list[2], (3, NX, NY, NZ), 0.7, 4.0, ((1, 8), (2, 4)), jnp.float32)
    pressure = jnp.clip(jnp.exp(math.log(2.0) - 2.3025851 * jax.random.uniform(key_list[3], (NX, NY, NZ), jnp.float32) ** levels(key_list[3], (NX, NY, NZ), ((0, 8), (1, 4)), -0.2, 0.2)), 0.2, 2.0)
    line_owner_keys = jax.random.split(jax.random.fold_in(key_list[4], 1), N_GX * N_PB * ROWS_DEV // ROWS_DEV)
    line_owner_turns = jax.random.permutation(jax.random.fold_in(key_list[4], 3), N_GX * N_PB * ROWS_DEV // ROWS_DEV)
    line_owner = jax.vmap(lambda own, number: routed_block(jax.random.fold_in(key_list[4], 2), own, number, ROWS_DEV, N_GX, 1, CAP, 2))(line_owner_keys, line_owner_turns).reshape((N_GX, N_PB, ROWS_DEV, 1))
    line_row = with_ends(jax.random.randint(key_list[5], (N_GX, N_PB, ROWS_DEV), 0, RI), jax.random.fold_in(key_list[5], 1), 0, RI - 1).astype(jnp.int32)
    pedersen = jnp.clip(jnp.exp(math.log(8.0) - 2.7725887 * jax.random.uniform(key_list[6], (NLAT, ILON), jnp.float32) ** levels(key_list[6], (NLAT, ILON), ((0, 32),), -0.2, 0.2)), 0.5, 8.0)
    hall = jnp.clip(jnp.exp(math.log(5.0) - 2.8134107 * jax.random.uniform(key_list[7], (NLAT, ILON), jnp.float32) ** levels(key_list[7], (NLAT, ILON), ((0, 32),), -0.2, 0.2)), 0.3, 5.0)
    mirror_shift = draw_mirror_shift(jax.random.fold_in(key_list[9], 71), 0)
    return dict(density=density, velocity=velocity, magnetic=magnetic, pressure=pressure, line_owner=line_owner, line_row=line_row, pedersen=pedersen, hall=hall, mirror_shift=mirror_shift)


GAMMA = 5.0 / 3.0
COURANT = 0.08

def spatial_slice(values, axis, start, stop):
    return lax.slice_in_dim(values, start, stop, axis=values.ndim - 3 + axis)

def conserved_of(density, velocity, magnetic, pressure):
    field_sq = lax.optimization_barrier(jnp.sum(magnetic * magnetic, axis=0))
    energy = pressure / (GAMMA - 1.0) + 0.5 * density * lax.optimization_barrier(jnp.sum(velocity * velocity, axis=0)) + 0.5 * field_sq
    return jnp.concatenate([density[None], density * velocity, magnetic, energy[None]], axis=0)

def direction_flux(density, velocity, magnetic, pressure, d):
    normal_v = velocity[d]
    normal_b = magnetic[d]
    field_sq = lax.optimization_barrier(jnp.sum(magnetic * magnetic, axis=0))
    total_p = pressure + 0.5 * field_sq
    energy = pressure / (GAMMA - 1.0) + 0.5 * density * lax.optimization_barrier(jnp.sum(velocity * velocity, axis=0)) + 0.5 * field_sq
    normal_unit = (jnp.arange(3) == d).astype(jnp.float32)[:, None, None, None]
    momentum = density * velocity * normal_v - magnetic * normal_b + normal_unit * total_p
    induced = magnetic * normal_v - normal_b * velocity
    v_dot_b = lax.optimization_barrier(jnp.sum(velocity * magnetic, axis=0))
    fluxes = jnp.concatenate([(density * normal_v)[None], momentum, induced, ((energy + total_p) * normal_v - normal_b * v_dot_b)[None]], axis=0)
    sound_sq = GAMMA * pressure / density
    alfven = field_sq / density
    spread = (sound_sq + alfven) ** 2 - 4.0 * sound_sq * normal_b * normal_b / density
    fast_speed = jnp.sqrt(0.5 * (sound_sq + alfven + jnp.sqrt(jnp.maximum(spread, 0.0))))
    return (fluxes, jnp.abs(normal_v) + fast_speed)

def advance(density, velocity, magnetic, pressure):
    conserved_state = conserved_of(density, velocity, magnetic, pressure)
    change = jnp.zeros_like(conserved_state[:, 1:-1, 1:-1, 1:-1])
    for d in range(3):
        fluxes, speeds = direction_flux(density, velocity, magnetic, pressure, d)
        n = density.shape[d]
        lower_flux = spatial_slice(fluxes, d, 0, n - 1)
        upper_flux = spatial_slice(fluxes, d, 1, n)
        lower_state = spatial_slice(conserved_state, d, 0, n - 1)
        upper_state = spatial_slice(conserved_state, d, 1, n)
        largest = jnp.maximum(spatial_slice(speeds, d, 0, n - 1), spatial_slice(speeds, d, 1, n))
        interface = 0.5 * (lower_flux + upper_flux) - 0.5 * largest * (upper_state - lower_state)
        divergence = spatial_slice(interface, d, 1, n - 1) - spatial_slice(interface, d, 0, n - 2)
        for e in range(3):
            if e != d:
                divergence = spatial_slice(divergence, e, 1, density.shape[e] - 1)
        change = change + divergence
    interior = conserved_state[:, 1:-1, 1:-1, 1:-1]
    return interior - COURANT * change

def derivative(values, axis):
    n = values.shape[axis]
    result = (lax.slice_in_dim(values, 2, n, axis=axis) - lax.slice_in_dim(values, 0, n - 2, axis=axis)) * 0.5
    for e in range(3):
        if e != axis:
            result = lax.slice_in_dim(result, 1, result.shape[e] - 1, axis=e)
    return result

def aligned_current(field_pad):
    field_x, field_y, field_z = (field_pad[0], field_pad[1], field_pad[2])
    current_x = derivative(field_z, 1) - derivative(field_y, 2)
    current_y = derivative(field_x, 2) - derivative(field_z, 0)
    current_z = derivative(field_y, 0) - derivative(field_x, 1)
    interior = field_pad[:, 1:-1, 1:-1, 1:-1]
    field_size = jnp.sqrt(lax.optimization_barrier(jnp.sum(interior * interior, axis=0)))
    along = current_x * interior[0] + current_y * interior[1] + current_z * interior[2]
    return along / jnp.maximum(field_size, 1.0)

def weights(pedersen_pad, hall_pad):
    pedersen = pedersen_pad[..., 1:-1, :]
    hall = hall_pad[..., 1:-1, :]
    up_ped = pedersen_pad[..., :-2, :]
    down_ped = pedersen_pad[..., 2:, :]
    up_hall = hall_pad[..., :-2, :]
    down_hall = hall_pad[..., 2:, :]
    up_weight = 0.5 * (pedersen + up_ped)
    down_weight = 0.5 * (pedersen + down_ped)
    east_weight = 0.5 * (pedersen + jnp.roll(pedersen, -1, axis=-1))
    west_weight = 0.5 * (pedersen + jnp.roll(pedersen, 1, axis=-1))
    up_east = 0.125 * (hall + jnp.roll(up_hall, -1, axis=-1))
    up_west = 0.125 * (hall + jnp.roll(up_hall, 1, axis=-1))
    down_east = 0.125 * (hall + jnp.roll(down_hall, -1, axis=-1))
    down_west = 0.125 * (hall + jnp.roll(down_hall, 1, axis=-1))
    center = up_weight + down_weight + east_weight + west_weight + up_east + up_west + down_east + down_west
    return (up_weight, down_weight, east_weight, west_weight, up_east, -up_west, -down_east, down_west, center)

def sweep(potential_pad, stencil, sources):
    up_weight, down_weight, east_weight, west_weight, up_east, up_west, down_east, down_west, center = stencil
    middle = potential_pad[..., 1:-1, :]
    upper = potential_pad[..., :-2, :]
    lower = potential_pad[..., 2:, :]
    summed = up_weight * upper + down_weight * lower
    summed = summed + east_weight * jnp.roll(middle, -1, axis=-1) + west_weight * jnp.roll(middle, 1, axis=-1)
    summed = summed + up_east * jnp.roll(upper, -1, axis=-1) + up_west * jnp.roll(upper, 1, axis=-1)
    summed = summed + down_east * jnp.roll(lower, -1, axis=-1) + down_west * jnp.roll(lower, 1, axis=-1)
    return (summed + sources) / center

def couple(local_phi, partner_phi, local_ped, partner_ped, shifts):
    n = local_phi.shape[-1]
    columns = (jnp.arange(n, dtype=jnp.int32)[None, :] + shifts[:, None]) % n
    mirrored = jnp.take_along_axis(partner_phi, columns, axis=-1)
    mirrored_ped = jnp.take_along_axis(partner_ped, columns, axis=-1)
    return (local_ped * local_phi + mirrored_ped * mirrored) / (local_ped + mirrored_ped)

def pad_edge(values):
    widths = [(0, 0)] * (values.ndim - 3) + [(1, 1)] * 3
    return jnp.pad(values, widths, mode='edge')

def reference(density, velocity, magnetic, pressure, line_owner, line_row, pedersen, hall, mirror_shift):
    density_pad = pad_edge(density)
    velocity_pad = pad_edge(velocity)
    magnetic_pad = pad_edge(magnetic)
    pressure_pad = pad_edge(pressure)

    def advance_plane(i):

        def window(values):
            return lax.dynamic_slice_in_dim(values, i, 3, axis=values.ndim - 3)
        return advance(window(density_pad), window(velocity_pad), window(magnetic_pad), window(pressure_pad))[:, 0]
    planes = lax.map(advance_plane, jnp.arange(NX, dtype=jnp.int32))
    updated = jnp.transpose(planes, (1, 0, 2, 3))
    current = aligned_current(pad_edge(updated[4:7]))
    current_rows = current.reshape(N_GX, CX, N_PB, CY, NZ).transpose(0, 2, 1, 3, 4).reshape(N_GX, N_PB, CX * CY, NZ)
    band_index = jnp.arange(N_PB, dtype=jnp.int32)[None, :, None]
    target = (line_owner[..., 0] * N_PB + band_index) * RI + line_row
    sources = jax.ops.segment_sum(current_rows.reshape(-1, NZ), target.reshape(-1), num_segments=NLAT)
    quarter = ILAT // 2

    def split_halves(values):
        return jnp.roll(values, quarter, axis=0).reshape((2, ILAT) + values.shape[1:])

    def zero_pad(values):
        return jnp.pad(values, ((0, 0), (1, 1), (0, 0)))
    pedersen_two = split_halves(pedersen)
    stencil = weights(zero_pad(pedersen_two), zero_pad(split_halves(hall)))
    sources_two = split_halves(sources)
    shifts = split_halves(mirror_shift)
    potential = jnp.zeros((2, ILAT, ILON), jnp.float32)
    for repeat in range(SWEEPS):
        potential = sweep(zero_pad(potential), stencil, sources_two)
        northern = couple(potential[0], potential[1], pedersen_two[0], pedersen_two[1], shifts[0])
        southern = couple(potential[1], potential[0], pedersen_two[1], pedersen_two[0], shifts[1])
        potential = jnp.stack([northern, southern])
    return (updated, jnp.roll(potential.reshape(NLAT, ILON), -quarter, axis=0))
```

```python
import functools

import jax
import jax.numpy as jnp
from jax import lax
from jax.experimental import pallas as pl
from jax.experimental.pallas import tpu as pltpu
from jax.sharding import PartitionSpec as P

SWEEPS = 8
GAMMA = 5.0 / 3.0
COURANT = 0.08
PAD = 8
F32 = jnp.float32
MESH = pl.DeviceIdType.MESH


def cell_terms(prim):
    rho, vel, mag, pres = prim[0], prim[1:4], prim[4:7], prim[7]
    field_sq = mag[0] * mag[0] + mag[1] * mag[1] + mag[2] * mag[2]
    vel_sq = vel[0] * vel[0] + vel[1] * vel[1] + vel[2] * vel[2]
    half_sq = 0.5 * field_sq
    energy = pres * (1.0 / (GAMMA - 1.0)) + 0.5 * rho * vel_sq + half_sq
    total_p = pres + half_sq
    v_dot_b = vel[0] * mag[0] + vel[1] * mag[1] + vel[2] * mag[2]
    inv = 1.0 / rho
    sound_sq = GAMMA * pres * inv
    both = sound_sq + field_sq * inv
    momentum = [rho * v for v in vel]
    state = [rho] + momentum + list(mag) + [energy]
    return state, total_p, v_dot_b, sound_sq * inv, both


def flux_of(prim, terms, d):
    state, total_p, v_dot_b, sound_over, both = terms
    vel, mag = prim[1:4], prim[4:7]
    vn, bn = vel[d], mag[d]
    flux = [state[1 + d]]
    for e in range(3):
        m = state[1 + e] * vn - mag[e] * bn
        flux.append(m + total_p if e == d else m)
    for e in range(3):
        flux.append(None if e == d else mag[e] * vn - bn * vel[e])
    flux.append((state[7] + total_p) * vn - bn * v_dot_b)
    spread = both * both - 4.0 * sound_over * bn * bn
    fast = jnp.sqrt(0.5 * (both + jnp.sqrt(jnp.maximum(spread, 0.0))))
    return flux, jnp.abs(vn) + fast


def face(f_lo, f_hi, u_lo, u_hi, largest):
    jump = largest * (u_hi - u_lo)
    return -0.5 * jump if f_lo is None else 0.5 * ((f_lo + f_hi) - jump)


def roll(values, shift, axis):
    return pltpu.roll(values, shift % values.shape[axis], axis)


def kernel(sizes, rho, vel, mag, pres, owner, line_row, ped, hall, shift,
           out, phi_out,
           win, fwin, part, part_in, cwin, swin, shwin,
           loc_sem, xs, xr, ys, yr, cs, cr, fs, fr, as_, ar, ss, sr):
    nx, ny = sizes
    cx, cy, nz = rho.shape
    ri = ped.shape[0]
    g, p = lax.axis_index("gx"), lax.axis_index("pb")
    n = nx * ny
    half = n // 2
    b = g * ny + p

    def dev(flat):
        return (flat // ny, flat % ny)

    ion = [
        ((b + 1) % n, 0),
        ((b + n - 1) % n, 2),
        ((b + half + 1) % n, 3),
        ((b + half) % n, 4),
        ((b + half + n - 1) % n, 5),
    ]

    barrier = pltpu.get_barrier_semaphore()

    def greet(k, carry):
        pl.semaphore_signal(barrier, inc=1, device_id=((g + k) % nx, p), device_id_type=MESH)
        return carry

    lax.fori_loop(1, nx, greet, 0)
    for flat, slot in ion:
        if slot != 4:
            pl.semaphore_signal(barrier, inc=1, device_id=dev(flat), device_id_type=MESH)

    rows = pl.ds(PAD, cy)
    mid = pl.ds(1, cx)
    prims = [(rho, 0, 1), (vel, 1, 3), (mag, 4, 3), (pres, 7, 1)]
    local = []
    for i, (ref, at, count) in enumerate(prims):
        dst = win.at[at] if count == 1 else win.at[pl.ds(at, count)]
        dst = dst.at[mid, rows] if count == 1 else dst.at[:, mid, rows]
        local.append(pltpu.make_async_copy(ref, dst, loc_sem.at[i]))
    cond_local = [
        pltpu.make_async_copy(ped, cwin.at[0, 1], loc_sem.at[4]),
        pltpu.make_async_copy(hall, cwin.at[1, 1], loc_sem.at[5]),
    ]
    for c in local + cond_local:
        c.start()

    row8 = lax.broadcasted_iota(jnp.int32, (ri, nz), 0)
    sh = jnp.zeros((ri, nz), jnp.int32)
    for i in range(ri):
        sh = jnp.where(row8 == i, shift[i], sh)
    shwin[1] = sh

    pl.semaphore_wait(barrier, nx - 1 + 4)

    def remote(src, dst, send, recv, where):
        return pltpu.make_async_remote_copy(
            src_ref=src, dst_ref=dst, send_sem=send, recv_sem=recv,
            device_id=where, device_id_type=MESH)

    x_up, x_dn = (jnp.minimum(g + 1, nx - 1), p), (jnp.maximum(g - 1, 0), p)
    y_up, y_dn = (g, jnp.minimum(p + 1, ny - 1)), (g, jnp.maximum(p - 1, 0))
    has_xu, has_xd, has_yu, has_yd = g < nx - 1, g > 0, p < ny - 1, p > 0

    def halo_copies(srcs, wref, sends, recvs, is_x):
        both = []
        for way in range(2):
            copies = []
            for i, (ref, at, count, lead) in enumerate(srcs):
                if is_x:
                    s_at = (cx - 1 if way == 0 else 0) + lead[0]
                    d_at = 0 if way == 0 else cx + 1
                    r = pl.ds(lead[1], cy)
                    if count == 1:
                        src, dst = ref.at[s_at, r], wref.at[at, d_at, rows]
                    else:
                        src = ref.at[pl.ds(lead[2], count), s_at, r]
                        dst = wref.at[pl.ds(at, count), d_at, rows]
                    where = x_up if way == 0 else x_dn
                else:
                    s_at = (cy - PAD if way == 0 else 0) + lead[1]
                    d_at = 0 if way == 0 else PAD + cy
                    xs_ = pl.ds(lead[0], cx)
                    if count == 1:
                        src = ref.at[xs_, pl.ds(s_at, PAD)]
                        dst = wref.at[at, mid, pl.ds(d_at, PAD)]
                    else:
                        src = ref.at[pl.ds(lead[2], count), xs_, pl.ds(s_at, PAD)]
                        dst = wref.at[pl.ds(at, count), mid, pl.ds(d_at, PAD)]
                    where = y_up if way == 0 else y_dn
                copies.append(remote(src, dst, sends.at[way, i], recvs.at[way, i], where))
            both.append(copies)
        return both

    def each(cond, copies, act):
        @pl.when(cond)
        def _():
            for c in copies:
                getattr(c, act)()

    srcs = [(ref, at, count, (0, 0, 0)) for ref, at, count in prims]
    xc = halo_copies(srcs, win, xs, xr, True)
    yc = halo_copies(srcs, win, ys, yr, False)
    each(has_xu, xc[0], "start")
    each(has_xd, xc[1], "start")
    each(has_yu, yc[0], "start")
    each(has_yd, yc[1], "start")
    cond_copies = []
    for flat, slot in ion:
        cond_copies.append(remote(ped, cwin.at[0, slot], cs.at[0, slot], cr.at[0, slot], dev(flat)))
        cond_copies.append(remote(hall, cwin.at[1, slot], cs.at[1, slot], cr.at[1, slot], dev(flat)))
        if slot < 3:
            cond_copies.append(
                remote(shwin.at[1], shwin.at[slot], cs.at[2, slot], cr.at[2, slot], dev(flat)))
    for c in cond_copies:
        c.start()

    for c in local + cond_local:
        c.wait()

    lane = lax.broadcasted_iota(jnp.int32, (cx, cy, nz), 2)
    prim = [win[v, 1:1 + cx, PAD:PAD + cy, :] for v in range(8)]
    terms = cell_terms(prim)
    flux, speed = flux_of(prim, terms, 2)
    first, last = lane == 0, lane == nz - 1

    def z_dn(a):
        return jnp.where(first, a, roll(a, 1, 2))

    largest = jnp.maximum(speed, z_dn(speed))
    for v in range(8):
        u, f = terms[0][v], flux[v]
        low = face(None if f is None else z_dn(f), f, z_dn(u), u, largest)
        top = jnp.zeros_like(u) if f is None else f
        high = jnp.where(last, top, roll(low, -1, 2))
        out[v] = u - COURANT * (high - low)

    each(has_yd, yc[0], "wait_recv")
    each(has_yu, yc[1], "wait_recv")

    @pl.when(p == 0)
    def _():
        for v in range(8):
            win[v, 1:1 + cx, PAD - 1:PAD, :] = win[v, 1:1 + cx, PAD:PAD + 1, :]

    @pl.when(p == ny - 1)
    def _():
        for v in range(8):
            win[v, 1:1 + cx, PAD + cy:PAD + cy + 1, :] = win[v, 1:1 + cx, PAD + cy - 1:PAD + cy, :]

    prim = [win[v, 1:1 + cx] for v in range(8)]
    terms = cell_terms(prim)
    flux, speed = flux_of(prim, terms, 1)
    largest = jnp.maximum(speed, roll(speed, 1, 1))
    for v in range(8):
        u, f = terms[0][v], flux[v]
        low = face(None if f is None else roll(f, 1, 1), f, roll(u, 1, 1), u, largest)
        diff = roll(low, -1, 1) - low
        out[v] = out[v] - COURANT * diff[:, PAD:PAD + cy, :]

    each(has_xd, xc[0], "wait_recv")
    each(has_xu, xc[1], "wait_recv")

    @pl.when(g == 0)
    def _():
        for v in range(8):
            win[v, 0, PAD:PAD + cy, :] = win[v, 1, PAD:PAD + cy, :]

    @pl.when(g == nx - 1)
    def _():
        for v in range(8):
            win[v, cx + 1, PAD:PAD + cy, :] = win[v, cx, PAD:PAD + cy, :]

    prim = [win[v, :, PAD:PAD + cy, :] for v in range(8)]
    terms = cell_terms(prim)
    flux, speed = flux_of(prim, terms, 0)
    largest = jnp.maximum(speed[:-1], speed[1:])
    for v in (4, 6, 5, 0, 1, 2, 3, 7):
        u, f = terms[0][v], flux[v]
        lows = face(None if f is None else f[:-1], None if f is None else f[1:], u[:-1], u[1:], largest)
        new = out[v] - COURANT * (lows[1:] - lows[:-1])
        out[v] = new
        if 4 <= v <= 6:
            fwin[{4: 0, 6: 1, 5: 2}[v], 1:1 + cx, PAD:PAD + cy, :] = new
        if v == 5:
            fx = halo_copies([(fwin, 1, 2, (1, PAD, 1))], fwin, fs.at[0], fr.at[0], True)
            fy = halo_copies([(fwin, 0, 2, (1, PAD, 0))], fwin, fs.at[1], fr.at[1], False)
            each(has_xu, fx[0], "start")
            each(has_xd, fx[1], "start")
            each(has_yu, fy[0], "start")
            each(has_yd, fy[1], "start")

    each(has_xd, fx[0], "wait_recv")
    each(has_xu, fx[1], "wait_recv")
    each(has_yd, fy[0], "wait_recv")
    each(has_yu, fy[1], "wait_recv")

    @pl.when(g == 0)
    def _():
        for v in (1, 2):
            fwin[v, 0, PAD:PAD + cy, :] = fwin[v, 1, PAD:PAD + cy, :]

    @pl.when(g == nx - 1)
    def _():
        for v in (1, 2):
            fwin[v, cx + 1, PAD:PAD + cy, :] = fwin[v, cx, PAD:PAD + cy, :]

    @pl.when(p == 0)
    def _():
        for v in (0, 1):
            fwin[v, 1:1 + cx, PAD - 1:PAD, :] = fwin[v, 1:1 + cx, PAD:PAD + 1, :]

    @pl.when(p == ny - 1)
    def _():
        for v in (0, 1):
            fwin[v, 1:1 + cx, PAD + cy:PAD + cy + 1, :] = (
                fwin[v, 1:1 + cx, PAD + cy - 1:PAD + cy, :])

    def d_x(v):
        return 0.5 * (fwin[v, 2:2 + cx, PAD:PAD + cy, :] - fwin[v, 0:cx, PAD:PAD + cy, :])

    def d_y(v):
        a = fwin[v, 1:1 + cx]
        return 0.5 * (roll(a, -1, 1) - roll(a, 1, 1))[:, PAD:PAD + cy, :]

    def d_z(a):
        return 0.5 * (jnp.where(last, a, roll(a, -1, 2)) - z_dn(a))

    bx, bz, by = [fwin[v, 1:1 + cx, PAD:PAD + cy, :] for v in range(3)]
    jx = d_y(1) - d_z(by)
    jy = d_z(bx) - d_x(1)
    jz = d_x(2) - d_y(0)
    size = jnp.sqrt(bx * bx + by * by + bz * bz)
    current = (jx * bx + jy * by + jz * bz) / jnp.maximum(size, 1.0)
    current = current.reshape(cx * cy, nz)

    owners = owner[0, 0]
    row_hot = (lax.broadcasted_iota(jnp.int32, (ri, cx * cy), 0) == line_row[0]).astype(F32)

    def send_part(o, at):
        return remote(part.at[o], part_in.at[at], as_.at[o], ar.at[at], (o, p))

    def deposit(k, carry):
        o = (g + k) % nx
        mine = jnp.where(owners == o, current, 0.0)
        part[o] = jnp.dot(row_hot, mine, precision=lax.Precision.HIGHEST,
                          preferred_element_type=F32)

        @pl.when(k < nx)
        def _():
            send_part(o, g).start()

        return carry

    lax.fori_loop(1, nx + 1, deposit, 0, unroll=nx <= 8)

    for c in cond_copies:
        c.wait_recv()
    wide = 6 * ri
    row = lax.broadcasted_iota(jnp.int32, (wide, nz), 0)
    row = jnp.where(row >= 3 * ri, row - 3 * ri, row)
    place = b % half
    low_row = jnp.where(place == half // 2, ri, 0)
    high_row = jnp.where(place == half // 2 - 1, 2 * ri, 3 * ri)
    valid = (row >= low_row) & (row < high_row)
    pw = jnp.where(valid, cwin[0].reshape(wide, nz), 0.0)
    hw = jnp.where(valid, cwin[1].reshape(wide, nz), 0.0)
    own_shift = shwin[...].reshape(3 * ri, nz)
    col = lax.broadcasted_iota(jnp.int32, (3 * ri, nz), 1)
    cols = jnp.concatenate(
        [(col + own_shift) % nz, (col + (nz - own_shift)) % nz], axis=0)

    def swap(a):
        other = jnp.concatenate([a[3 * ri:], a[:3 * ri]], axis=0)
        return jnp.take_along_axis(other, cols, axis=1)

    def east(a):
        return roll(a, -1, 1)

    def west(a):
        return roll(a, 1, 1)

    def up(a):
        return roll(a, 1, 0)

    def down(a):
        return roll(a, -1, 0)

    he, hwst = east(hw), west(hw)
    coef = [
        0.5 * (pw + up(pw)), 0.5 * (pw + down(pw)),
        0.5 * (pw + east(pw)), 0.5 * (pw + west(pw)),
        0.125 * (hw + up(he)), 0.125 * (hw + up(hwst)),
        0.125 * (hw + down(he)), 0.125 * (hw + down(hwst)),
    ]
    center = coef[0]
    for c in coef[1:]:
        center = center + c
    inv = jnp.where(valid, 1.0 / jnp.where(valid, center, 1.0), 0.0)
    cu, cd, ce, cw, cue, cuw, cde, cdw = [c * inv for c in coef]
    pm = swap(pw)
    both = jnp.where(valid, pw + pm, 1.0)
    wa = jnp.where(valid, pw / both, 0.0)
    wb = jnp.where(valid, pm / both, 0.0)

    def take_part(k, total):
        s = (g + k) % nx
        send_part(s, s).wait_recv()
        return total + part_in[s]

    total = lax.fori_loop(1, nx, take_part, part[g], unroll=nx <= 8)
    swin[1] = total
    s_copies = [
        remote(swin.at[1], swin.at[slot], ss.at[slot], sr.at[slot], dev(flat)) for flat, slot in ion]
    for c in s_copies:
        c.start()
    for c in s_copies:
        c.wait_recv()
    source = swin[...].reshape(wide, nz) * inv

    def couple(phi):
        return wa * phi + wb * swap(phi)

    phi = couple(source)
    for _ in range(SWEEPS - 1):
        e, w = east(phi), west(phi)
        acc = source + ce * e + cw * w
        acc = acc + up_terms(phi, e, w, cu, cue, cuw, up)
        acc = acc + up_terms(phi, e, w, cd, -cde, -cdw, down)
        phi = couple(acc)
    phi_out[...] = phi[ri:2 * ri]

    each(has_xu, xc[0] + fx[0], "wait_send")
    each(has_xd, xc[1] + fx[1], "wait_send")
    each(has_yu, yc[0] + fy[0], "wait_send")
    each(has_yd, yc[1] + fy[1], "wait_send")
    for c in cond_copies + s_copies:
        c.wait_send()

    def sent(k, carry):
        send_part((g + k) % nx, g).wait_send()
        return carry

    lax.fori_loop(1, nx, sent, 0)


def up_terms(phi, e, w, straight, plus, minus, move):
    return straight * move(phi) + plus * move(e) - minus * move(w)


def body(sizes, density, velocity, magnetic, pressure, line_owner, line_row, pedersen, hall, mirror_shift):
    cx, cy, nz = density.shape
    ri = pedersen.shape[0]
    nx = sizes[0]
    any_ = pl.BlockSpec(memory_space=pl.ANY)
    vmem = pl.BlockSpec(memory_space=pltpu.VMEM)
    smem = pl.BlockSpec(memory_space=pltpu.SMEM)
    dma = pltpu.SemaphoreType.DMA
    return pl.pallas_call(
        functools.partial(kernel, sizes),
        out_shape=(
            jax.ShapeDtypeStruct((8, cx, cy, nz), F32),
            jax.ShapeDtypeStruct((ri, nz), F32),
        ),
        in_specs=[any_] * 4 + [vmem] * 2 + [any_] * 2 + [smem],
        out_specs=(vmem, vmem),
        scratch_shapes=[
            pltpu.VMEM((8, cx + 2, cy + 2 * PAD, nz), F32),
            pltpu.VMEM((3, cx + 2, cy + 2 * PAD, nz), F32),
            pltpu.VMEM((nx, ri, nz), F32),
            pltpu.VMEM((nx, ri, nz), F32),
            pltpu.VMEM((2, 6, ri, nz), F32),
            pltpu.VMEM((6, ri, nz), F32),
            pltpu.VMEM((3, ri, nz), jnp.int32),
            dma((6,)),
            dma((2, 4)), dma((2, 4)), dma((2, 4)), dma((2, 4)),
            dma((3, 6)), dma((3, 6)),
            dma((2, 2, 1)), dma((2, 2, 1)),
            dma((nx,)), dma((nx,)),
            dma((6,)), dma((6,)),
        ],
        compiler_params=pltpu.CompilerParams(collective_id=0, has_side_effects=True),
        name="flux_and_potential",
    )(density, velocity, magnetic, pressure, line_owner, line_row, pedersen, hall, mirror_shift)


def solution(mesh):
    sizes = (mesh.shape["gx"], mesh.shape["pb"])
    in_specs = (
        P("gx", "pb", None),
        P(None, "gx", "pb", None),
        P(None, "gx", "pb", None),
        P("gx", "pb", None),
        P("gx", "pb", None, None),
        P("gx", "pb", None),
        P(("gx", "pb"), None),
        P(("gx", "pb"), None),
        P(("gx", "pb")),
    )
    out_specs = (P(None, "gx", "pb", None), P(("gx", "pb"), None))
    return jax.shard_map(
        functools.partial(body, sizes), mesh=mesh, in_specs=in_specs, out_specs=out_specs,
        check_vma=False)
```

```python
import functools

import jax
import jax.numpy as jnp
from jax import lax
from jax.experimental import pallas as pl
from jax.experimental.pallas import tpu as pltpu
from jax.sharding import PartitionSpec as P

SWEEPS = 8
GAMMA = 5.0 / 3.0
COURANT = 0.08
PAD = 8
F32 = jnp.float32
MESH = pl.DeviceIdType.MESH


def cell_terms(prim):
    rho, vel, mag, pres = prim[0], prim[1:4], prim[4:7], prim[7]
    field_sq = mag[0] * mag[0] + mag[1] * mag[1] + mag[2] * mag[2]
    vel_sq = vel[0] * vel[0] + vel[1] * vel[1] + vel[2] * vel[2]
    half_sq = 0.5 * field_sq
    energy = pres * (1.0 / (GAMMA - 1.0)) + 0.5 * rho * vel_sq + half_sq
    total_p = pres + half_sq
    v_dot_b = vel[0] * mag[0] + vel[1] * mag[1] + vel[2] * mag[2]
    inv = 1.0 / rho
    sound_sq = GAMMA * pres * inv
    both = sound_sq + field_sq * inv
    momentum = [rho * v for v in vel]
    state = [rho] + momentum + list(mag) + [energy]
    return state, total_p, v_dot_b, sound_sq * inv, both


def flux_of(prim, terms, d):
    state, total_p, v_dot_b, sound_over, both = terms
    vel, mag = prim[1:4], prim[4:7]
    vn, bn = vel[d], mag[d]
    flux = [state[1 + d]]
    for e in range(3):
        m = state[1 + e] * vn - mag[e] * bn
        flux.append(m + total_p if e == d else m)
    for e in range(3):
        flux.append(None if e == d else mag[e] * vn - bn * vel[e])
    flux.append((state[7] + total_p) * vn - bn * v_dot_b)
    spread = both * both - 4.0 * sound_over * bn * bn
    fast = jnp.sqrt(0.5 * (both + jnp.sqrt(jnp.maximum(spread, 0.0))))
    return flux, jnp.abs(vn) + fast


def face(f_lo, f_hi, u_lo, u_hi, largest):
    jump = largest * (u_hi - u_lo)
    return -0.5 * jump if f_lo is None else 0.5 * ((f_lo + f_hi) - jump)


def roll(values, shift, axis):
    return pltpu.roll(values, shift % values.shape[axis], axis)


def kernel(sizes, rho, vel, mag, pres, owner, line_row, ped, hall, shift,
           out, phi_out,
           win, fwin, part, part_in, cwin, swin, shwin,
           loc_sem, xs, xr, ys, yr, cs, cr, fs, fr, as_, ar, ss, sr):
    nx, ny = sizes
    cx, cy, nz = rho.shape
    ri = ped.shape[0]
    g, p = lax.axis_index("gx"), lax.axis_index("pb")
    n = nx * ny
    half = n // 2
    b = g * ny + p

    def dev(flat):
        return (flat // ny, flat % ny)

    ion = [
        ((b + 1) % n, 0),
        ((b + n - 1) % n, 2),
        ((b + half + 1) % n, 3),
        ((b + half) % n, 4),
        ((b + half + n - 1) % n, 5),
    ]

    barrier = pltpu.get_barrier_semaphore()

    def greet(k, carry):
        pl.semaphore_signal(barrier, inc=1, device_id=((g + k) % nx, p), device_id_type=MESH)
        return carry

    lax.fori_loop(1, nx, greet, 0)
    for flat, slot in ion:
        if slot != 4:
            pl.semaphore_signal(barrier, inc=1, device_id=dev(flat), device_id_type=MESH)

    rows = pl.ds(PAD, cy)
    mid = pl.ds(1, cx)
    prims = [(rho, 0, 1), (vel, 1, 3), (mag, 4, 3), (pres, 7, 1)]
    local = []
    for i, (ref, at, count) in enumerate(prims):
        dst = win.at[at] if count == 1 else win.at[pl.ds(at, count)]
        dst = dst.at[mid, rows] if count == 1 else dst.at[:, mid, rows]
        local.append(pltpu.make_async_copy(ref, dst, loc_sem.at[i]))
    cond_local = [
        pltpu.make_async_copy(ped, cwin.at[0, 1], loc_sem.at[4]),
        pltpu.make_async_copy(hall, cwin.at[1, 1], loc_sem.at[5]),
    ]
    for c in local + cond_local:
        c.start()

    row8 = lax.broadcasted_iota(jnp.int32, (ri, nz), 0)
    sh = jnp.zeros((ri, nz), jnp.int32)
    for i in range(ri):
        sh = jnp.where(row8 == i, shift[i], sh)
    shwin[1] = sh

    pl.semaphore_wait(barrier, nx - 1 + 4)

    def remote(src, dst, send, recv, where):
        return pltpu.make_async_remote_copy(
            src_ref=src, dst_ref=dst, send_sem=send, recv_sem=recv,
            device_id=where, device_id_type=MESH)

    x_up, x_dn = (jnp.minimum(g + 1, nx - 1), p), (jnp.maximum(g - 1, 0), p)
    y_up, y_dn = (g, jnp.minimum(p + 1, ny - 1)), (g, jnp.maximum(p - 1, 0))
    has_xu, has_xd, has_yu, has_yd = g < nx - 1, g > 0, p < ny - 1, p > 0

    def halo_copies(srcs, wref, sends, recvs, is_x):
        both = []
        for way in range(2):
            copies = []
            for i, (ref, at, count, lead) in enumerate(srcs):
                if is_x:
                    s_at = (cx - 1 if way == 0 else 0) + lead[0]
                    d_at = 0 if way == 0 else cx + 1
                    r = pl.ds(lead[1], cy)
                    if count == 1:
                        src, dst = ref.at[s_at, r], wref.at[at, d_at, rows]
                    else:
                        src = ref.at[pl.ds(lead[2], count), s_at, r]
                        dst = wref.at[pl.ds(at, count), d_at, rows]
                    where = x_up if way == 0 else x_dn
                else:
                    s_at = (cy - PAD if way == 0 else 0) + lead[1]
                    d_at = 0 if way == 0 else PAD + cy
                    xs_ = pl.ds(lead[0], cx)
                    if count == 1:
                        src = ref.at[xs_, pl.ds(s_at, PAD)]
                        dst = wref.at[at, mid, pl.ds(d_at, PAD)]
                    else:
                        src = ref.at[pl.ds(lead[2], count), xs_, pl.ds(s_at, PAD)]
                        dst = wref.at[pl.ds(at, count), mid, pl.ds(d_at, PAD)]
                    where = y_up if way == 0 else y_dn
                copies.append(remote(src, dst, sends.at[way, i], recvs.at[way, i], where))
            both.append(copies)
        return both

    def each(cond, copies, act):
        @pl.when(cond)
        def _():
            for c in copies:
                getattr(c, act)()

    srcs = [(ref, at, count, (0, 0, 0)) for ref, at, count in prims]
    xc = halo_copies(srcs, win, xs, xr, True)
    yc = halo_copies(srcs, win, ys, yr, False)
    each(has_xu, xc[0], "start")
    each(has_xd, xc[1], "start")
    each(has_yu, yc[0], "start")
    each(has_yd, yc[1], "start")
    cond_copies = []
    for flat, slot in ion:
        cond_copies.append(remote(ped, cwin.at[0, slot], cs.at[0, slot], cr.at[0, slot], dev(flat)))
        cond_copies.append(remote(hall, cwin.at[1, slot], cs.at[1, slot], cr.at[1, slot], dev(flat)))
        if slot < 3:
            cond_copies.append(
                remote(shwin.at[1], shwin.at[slot], cs.at[2, slot], cr.at[2, slot], dev(flat)))
    for c in cond_copies:
        c.start()

    for c in local + cond_local:
        c.wait()

    lane = lax.broadcasted_iota(jnp.int32, (cx, cy, nz), 2)
    prim = [win[v, 1:1 + cx, PAD:PAD + cy, :] for v in range(8)]
    terms = cell_terms(prim)
    flux, speed = flux_of(prim, terms, 2)
    first, last = lane == 0, lane == nz - 1

    def z_dn(a):
        return jnp.where(first, a, roll(a, 1, 2))

    largest = jnp.maximum(speed, z_dn(speed))
    for v in range(8):
        u, f = terms[0][v], flux[v]
        low = face(None if f is None else z_dn(f), f, z_dn(u), u, largest)
        top = jnp.zeros_like(u) if f is None else f
        high = jnp.where(last, top, roll(low, -1, 2))
        out[v] = u - COURANT * (high - low)

    each(has_yd, yc[0], "wait_recv")
    each(has_yu, yc[1], "wait_recv")

    @pl.when(p == 0)
    def _():
        for v in range(8):
            win[v, 1:1 + cx, PAD - 1:PAD, :] = win[v, 1:1 + cx, PAD:PAD + 1, :]

    @pl.when(p == ny - 1)
    def _():
        for v in range(8):
            win[v, 1:1 + cx, PAD + cy:PAD + cy + 1, :] = win[v, 1:1 + cx, PAD + cy - 1:PAD + cy, :]

    prim = [win[v, 1:1 + cx] for v in range(8)]
    terms = cell_terms(prim)
    flux, speed = flux_of(prim, terms, 1)
    largest = jnp.maximum(speed, roll(speed, 1, 1))
    for v in range(8):
        u, f = terms[0][v], flux[v]
        low = face(None if f is None else roll(f, 1, 1), f, roll(u, 1, 1), u, largest)
        diff = roll(low, -1, 1) - low
        out[v] = out[v] - COURANT * diff[:, PAD:PAD + cy, :]

    each(has_xd, xc[0], "wait_recv")
    each(has_xu, xc[1], "wait_recv")

    @pl.when(g == 0)
    def _():
        for v in range(8):
            win[v, 0, PAD:PAD + cy, :] = win[v, 1, PAD:PAD + cy, :]

    @pl.when(g == nx - 1)
    def _():
        for v in range(8):
            win[v, cx + 1, PAD:PAD + cy, :] = win[v, cx, PAD:PAD + cy, :]

    prim = [win[v, :, PAD:PAD + cy, :] for v in range(8)]
    terms = cell_terms(prim)
    flux, speed = flux_of(prim, terms, 0)
    largest = jnp.maximum(speed[:-1], speed[1:])
    for v in (4, 6, 5, 0, 1, 2, 3, 7):
        u, f = terms[0][v], flux[v]
        lows = face(None if f is None else f[:-1], None if f is None else f[1:], u[:-1], u[1:], largest)
        new = out[v] - COURANT * (lows[1:] - lows[:-1])
        out[v] = new
        if 4 <= v <= 6:
            fwin[{4: 0, 6: 1, 5: 2}[v], 1:1 + cx, PAD:PAD + cy, :] = new
        if v == 5:
            fx = halo_copies([(fwin, 1, 2, (1, PAD, 1))], fwin, fs.at[0], fr.at[0], True)
            fy = halo_copies([(fwin, 0, 2, (1, PAD, 0))], fwin, fs.at[1], fr.at[1], False)
            each(has_xu, fx[0], "start")
            each(has_xd, fx[1], "start")
            each(has_yu, fy[0], "start")
            each(has_yd, fy[1], "start")

    each(has_xd, fx[0], "wait_recv")
    each(has_xu, fx[1], "wait_recv")
    each(has_yd, fy[0], "wait_recv")
    each(has_yu, fy[1], "wait_recv")

    @pl.when(g == 0)
    def _():
        for v in (1, 2):
            fwin[v, 0, PAD:PAD + cy, :] = fwin[v, 1, PAD:PAD + cy, :]

    @pl.when(g == nx - 1)
    def _():
        for v in (1, 2):
            fwin[v, cx + 1, PAD:PAD + cy, :] = fwin[v, cx, PAD:PAD + cy, :]

    @pl.when(p == 0)
    def _():
        for v in (0, 1):
            fwin[v, 1:1 + cx, PAD - 1:PAD, :] = fwin[v, 1:1 + cx, PAD:PAD + 1, :]

    @pl.when(p == ny - 1)
    def _():
        for v in (0, 1):
            fwin[v, 1:1 + cx, PAD + cy:PAD + cy + 1, :] = (
                fwin[v, 1:1 + cx, PAD + cy - 1:PAD + cy, :])

    def d_x(v):
        return 0.5 * (fwin[v, 2:2 + cx, PAD:PAD + cy, :] - fwin[v, 0:cx, PAD:PAD + cy, :])

    def d_y(v):
        a = fwin[v, 1:1 + cx]
        return 0.5 * (roll(a, -1, 1) - roll(a, 1, 1))[:, PAD:PAD + cy, :]

    def d_z(a):
        return 0.5 * (jnp.where(last, a, roll(a, -1, 2)) - z_dn(a))

    bx, bz, by = [fwin[v, 1:1 + cx, PAD:PAD + cy, :] for v in range(3)]
    jx = d_y(1) - d_z(by)
    jy = d_z(bx) - d_x(1)
    jz = d_x(2) - d_y(0)
    size = jnp.sqrt(bx * bx + by * by + bz * bz)
    current = (jx * bx + jy * by + jz * bz) / jnp.maximum(size, 1.0)
    current = current.reshape(cx * cy, nz)

    pairs = nx // 2
    key = owner[0] * ri + line_row[0]
    pair_row = lax.broadcasted_iota(jnp.int32, (2 * ri, cx * cy), 0)
    pair_row = jnp.where(pair_row >= ri, pair_row + (pairs - 1) * ri, pair_row)

    def deposit(q, carry):
        hot = (key == pair_row + q * ri).astype(F32)
        part[q] = jnp.dot(hot, current, precision=lax.Precision.HIGHEST,
                          preferred_element_type=F32).reshape(2, ri, nz)
        return carry

    def send_part(o, at):
        return remote(part.at[o % pairs], part_in.at[at], as_.at[o], ar.at[at], (o, p))

    def send(k, carry):
        send_part((g + k) % nx, g).start()
        return carry

    lax.fori_loop(0, pairs, deposit, 0, unroll=nx <= 8)
    lax.fori_loop(1, nx, send, 0, unroll=nx <= 8)

    for c in cond_copies:
        c.wait_recv()
    wide = 6 * ri
    row = lax.broadcasted_iota(jnp.int32, (wide, nz), 0)
    row = jnp.where(row >= 3 * ri, row - 3 * ri, row)
    place = b % half
    low_row = jnp.where(place == half // 2, ri, 0)
    high_row = jnp.where(place == half // 2 - 1, 2 * ri, 3 * ri)
    valid = (row >= low_row) & (row < high_row)
    pw = jnp.where(valid, cwin[0].reshape(wide, nz), 0.0)
    hw = jnp.where(valid, cwin[1].reshape(wide, nz), 0.0)
    own_shift = shwin[...].reshape(3 * ri, nz)
    col = lax.broadcasted_iota(jnp.int32, (3 * ri, nz), 1)
    cols = jnp.concatenate(
        [(col + own_shift) % nz, (col + (nz - own_shift)) % nz], axis=0)

    def swap(a):
        other = jnp.concatenate([a[3 * ri:], a[:3 * ri]], axis=0)
        return jnp.take_along_axis(other, cols, axis=1)

    def east(a):
        return roll(a, -1, 1)

    def west(a):
        return roll(a, 1, 1)

    def up(a):
        return roll(a, 1, 0)

    def down(a):
        return roll(a, -1, 0)

    he, hwst = east(hw), west(hw)
    coef = [
        0.5 * (pw + up(pw)), 0.5 * (pw + down(pw)),
        0.5 * (pw + east(pw)), 0.5 * (pw + west(pw)),
        0.125 * (hw + up(he)), 0.125 * (hw + up(hwst)),
        0.125 * (hw + down(he)), 0.125 * (hw + down(hwst)),
    ]
    center = coef[0]
    for c in coef[1:]:
        center = center + c
    inv = jnp.where(valid, 1.0 / jnp.where(valid, center, 1.0), 0.0)
    cu, cd, ce, cw, cue, cuw, cde, cdw = [c * inv for c in coef]
    pm = swap(pw)
    both = jnp.where(valid, pw + pm, 1.0)
    wa = jnp.where(valid, pw / both, 0.0)
    wb = jnp.where(valid, pm / both, 0.0)

    def take_part(k, total):
        s = (g + k) % nx
        send_part(s, s).wait_recv()
        return total + part_in[s]

    total = lax.fori_loop(1, nx, take_part, part[g % pairs], unroll=nx <= 8)
    northern = g < pairs
    swin[0, 1] = jnp.where(northern, total[0], total[1])
    swin[1, 1] = jnp.where(northern, total[1], total[0])
    s_copies = [
        remote(swin.at[:, 1], swin.at[:, slot], ss.at[slot // 2], sr.at[slot // 2], dev(flat))
        for flat, slot in ion[:2]]
    for c in s_copies:
        c.start()
    for c in s_copies:
        c.wait_recv()
    source = swin[...].reshape(wide, nz) * inv

    def couple(phi):
        return wa * phi + wb * swap(phi)

    phi = couple(source)
    for _ in range(SWEEPS - 1):
        e, w = east(phi), west(phi)
        acc = source + ce * e + cw * w
        acc = acc + up_terms(phi, e, w, cu, cue, cuw, up)
        acc = acc + up_terms(phi, e, w, cd, -cde, -cdw, down)
        phi = couple(acc)
    phi_out[...] = phi[ri:2 * ri]

    each(has_xu, xc[0] + fx[0], "wait_send")
    each(has_xd, xc[1] + fx[1], "wait_send")
    each(has_yu, yc[0] + fy[0], "wait_send")
    each(has_yd, yc[1] + fy[1], "wait_send")
    for c in cond_copies + s_copies:
        c.wait_send()

    def sent(k, carry):
        send_part((g + k) % nx, g).wait_send()
        return carry

    lax.fori_loop(1, nx, sent, 0)


def up_terms(phi, e, w, straight, plus, minus, move):
    return straight * move(phi) + plus * move(e) - minus * move(w)


def body(sizes, density, velocity, magnetic, pressure, line_owner, line_row, pedersen, hall, mirror_shift):
    cx, cy, nz = density.shape
    ri = pedersen.shape[0]
    nx = sizes[0]
    any_ = pl.BlockSpec(memory_space=pl.ANY)
    vmem = pl.BlockSpec(memory_space=pltpu.VMEM)
    smem = pl.BlockSpec(memory_space=pltpu.SMEM)
    dma = pltpu.SemaphoreType.DMA
    return pl.pallas_call(
        functools.partial(kernel, sizes),
        out_shape=(
            pltpu.VMEM((8, cx, cy, nz), F32),
            pltpu.VMEM((ri, nz), F32),
        ),
        in_specs=[any_] * 4 + [vmem] * 2 + [any_] * 2 + [smem],
        out_specs=(vmem, vmem),
        scratch_shapes=[
            pltpu.VMEM((8, cx + 2, cy + 2 * PAD, nz), F32),
            pltpu.VMEM((3, cx + 2, cy + 2 * PAD, nz), F32),
            pltpu.VMEM((nx // 2, 2, ri, nz), F32),
            pltpu.VMEM((nx, 2, ri, nz), F32),
            pltpu.VMEM((2, 6, ri, nz), F32),
            pltpu.VMEM((2, 3, ri, nz), F32),
            pltpu.VMEM((3, ri, nz), jnp.int32),
            dma((6,)),
            dma((2, 4)), dma((2, 4)), dma((2, 4)), dma((2, 4)),
            dma((3, 6)), dma((3, 6)),
            dma((2, 2, 1)), dma((2, 2, 1)),
            dma((nx,)), dma((nx,)),
            dma((2,)), dma((2,)),
        ],
        compiler_params=pltpu.CompilerParams(collective_id=0, has_side_effects=True),
        name="flux_and_potential",
    )(density, velocity, magnetic, pressure, line_owner.reshape(1, 1, cx * cy), line_row, pedersen, hall, mirror_shift)


def solution(mesh):
    sizes = (mesh.shape["gx"], mesh.shape["pb"])
    in_specs = (
        P("gx", "pb", None),
        P(None, "gx", "pb", None),
        P(None, "gx", "pb", None),
        P("gx", "pb", None),
        P("gx", "pb", None, None),
        P("gx", "pb", None),
        P(("gx", "pb"), None),
        P(("gx", "pb"), None),
        P(("gx", "pb")),
    )
    out_specs = (P(None, "gx", "pb", None), P(("gx", "pb"), None))
    return jax.shard_map(
        functools.partial(body, sizes), mesh=mesh, in_specs=in_specs, out_specs=out_specs,
        check_vma=False)
```

```python
import functools

import jax
import jax.numpy as jnp
from jax import lax
from jax.experimental import pallas as pl
from jax.experimental.pallas import tpu as pltpu
from jax.sharding import PartitionSpec as P

SWEEPS = 8
GAMMA = 5.0 / 3.0
COURANT = 0.08
PAD = 8
F32 = jnp.float32
MESH = pl.DeviceIdType.MESH


def cell_terms(prim):
    rho, vel, mag, pres = prim[0], prim[1:4], prim[4:7], prim[7]
    field_sq = mag[0] * mag[0] + mag[1] * mag[1] + mag[2] * mag[2]
    vel_sq = vel[0] * vel[0] + vel[1] * vel[1] + vel[2] * vel[2]
    half_sq = 0.5 * field_sq
    energy = pres * (1.0 / (GAMMA - 1.0)) + 0.5 * rho * vel_sq + half_sq
    total_p = pres + half_sq
    v_dot_b = vel[0] * mag[0] + vel[1] * mag[1] + vel[2] * mag[2]
    inv = 1.0 / rho
    sound_sq = GAMMA * pres * inv
    both = sound_sq + field_sq * inv
    momentum = [rho * v for v in vel]
    state = [rho] + momentum + list(mag) + [energy]
    return state, total_p, v_dot_b, sound_sq * inv, both


def flux_of(prim, terms, d):
    state, total_p, v_dot_b = terms[:3]
    vel, mag = prim[1:4], prim[4:7]
    vn, bn = vel[d], mag[d]
    flux = [state[1 + d]]
    for e in range(3):
        m = state[1 + e] * vn - mag[e] * bn
        flux.append(m + total_p if e == d else m)
    for e in range(3):
        flux.append(None if e == d else mag[e] * vn - bn * vel[e])
    flux.append((state[7] + total_p) * vn - bn * v_dot_b)
    return flux


def speed_of(prim, terms, d):
    sound_over, both = terms[3:]
    vn, bn = prim[1 + d], prim[4 + d]
    spread = both * both - 4.0 * sound_over * bn * bn
    fast = jnp.sqrt(0.5 * (both + jnp.sqrt(jnp.maximum(spread, 0.0))))
    return jnp.abs(vn) + fast


def face(f_lo, f_hi, u_lo, u_hi, largest):
    jump = largest * (u_hi - u_lo)
    return -0.5 * jump if f_lo is None else 0.5 * ((f_lo + f_hi) - jump)


def roll(values, shift, axis):
    return pltpu.roll(values, shift % values.shape[axis], axis)


def kernel(sizes, rho, vel, mag, pres, owner, line_row, ped, hall, shift,
           out, phi_out,
           win, fwin, part, part_in, cwin, swin, shwin,
           loc_sem, xs, xr, ys, yr, cs, cr, fs, fr, as_, ar, ss, sr):
    nx, ny = sizes
    cx, cy, nz = rho.shape
    ri = ped.shape[0]
    g, p = lax.axis_index("gx"), lax.axis_index("pb")
    n = nx * ny
    half = n // 2
    b = g * ny + p

    def dev(flat):
        return (flat // ny, flat % ny)

    ion = [
        ((b + 1) % n, 0),
        ((b + n - 1) % n, 2),
        ((b + half + 1) % n, 3),
        ((b + half) % n, 4),
        ((b + half + n - 1) % n, 5),
    ]

    barrier = pltpu.get_barrier_semaphore()

    def greet(k, carry):
        pl.semaphore_signal(barrier, inc=1, device_id=((g + k) % nx, p), device_id_type=MESH)
        return carry

    lax.fori_loop(1, nx, greet, 0)
    for flat, slot in ion:
        if slot != 4:
            pl.semaphore_signal(barrier, inc=1, device_id=dev(flat), device_id_type=MESH)

    rows = pl.ds(PAD, cy)
    mid = pl.ds(1, cx)
    prims = [(rho, 0, 1), (vel, 1, 3), (mag, 4, 3), (pres, 7, 1)]
    local = []
    for i, (ref, at, count) in enumerate(prims):
        dst = win.at[at] if count == 1 else win.at[pl.ds(at, count)]
        dst = dst.at[mid, rows] if count == 1 else dst.at[:, mid, rows]
        local.append(pltpu.make_async_copy(ref, dst, loc_sem.at[i]))
    cond_local = [
        pltpu.make_async_copy(ped, cwin.at[0, 1], loc_sem.at[4]),
        pltpu.make_async_copy(hall, cwin.at[1, 1], loc_sem.at[5]),
    ]
    for c in local + cond_local:
        c.start()

    row8 = lax.broadcasted_iota(jnp.int32, (ri, nz), 0)
    sh = jnp.zeros((ri, nz), jnp.int32)
    for i in range(ri):
        sh = jnp.where(row8 == i, shift[i], sh)
    shwin[1] = sh

    pl.semaphore_wait(barrier, nx - 1 + 4)

    def remote(src, dst, send, recv, where):
        return pltpu.make_async_remote_copy(
            src_ref=src, dst_ref=dst, send_sem=send, recv_sem=recv,
            device_id=where, device_id_type=MESH)

    x_up, x_dn = (jnp.minimum(g + 1, nx - 1), p), (jnp.maximum(g - 1, 0), p)
    y_up, y_dn = (g, jnp.minimum(p + 1, ny - 1)), (g, jnp.maximum(p - 1, 0))
    has_xu, has_xd, has_yu, has_yd = g < nx - 1, g > 0, p < ny - 1, p > 0

    def halo_copies(srcs, wref, sends, recvs, is_x, first_sem=0):
        both = []
        for way in range(2):
            copies = []
            for i, (ref, at, count, lead) in enumerate(srcs, first_sem):
                if is_x:
                    s_at = (cx - 1 if way == 0 else 0) + lead[0]
                    d_at = 0 if way == 0 else cx + 1
                    r = pl.ds(lead[1], cy)
                    if count == 1:
                        src, dst = ref.at[s_at, r], wref.at[at, d_at, rows]
                    else:
                        src = ref.at[pl.ds(lead[2], count), s_at, r]
                        dst = wref.at[pl.ds(at, count), d_at, rows]
                    where = x_up if way == 0 else x_dn
                else:
                    s_at = (cy - PAD if way == 0 else 0) + lead[1]
                    d_at = 0 if way == 0 else PAD + cy
                    xs_ = pl.ds(lead[0], cx)
                    if count == 1:
                        src = ref.at[xs_, pl.ds(s_at, PAD)]
                        dst = wref.at[at, mid, pl.ds(d_at, PAD)]
                    else:
                        src = ref.at[pl.ds(lead[2], count), xs_, pl.ds(s_at, PAD)]
                        dst = wref.at[pl.ds(at, count), mid, pl.ds(d_at, PAD)]
                    where = y_up if way == 0 else y_dn
                copies.append(remote(src, dst, sends.at[way, i], recvs.at[way, i], where))
            both.append(copies)
        return both

    def each(cond, copies, act):
        @pl.when(cond)
        def _():
            for c in copies:
                getattr(c, act)()

    srcs = [(ref, at, count, (0, 0, 0)) for ref, at, count in prims]
    xc = halo_copies(srcs[1:3], win, xs, xr, True)
    xspeed = halo_copies([(win.at[8], 8, 1, (1, PAD, 0))], win, xs, xr, True, 2)
    xlate = halo_copies([srcs[0], srcs[3]], win, xs, xr, True, 3)
    yc = halo_copies(srcs, win, ys, yr, False)
    each(has_xu, xc[0], "start")
    each(has_xd, xc[1], "start")
    each(has_yu, yc[0], "start")
    each(has_yd, yc[1], "start")
    cond_copies = []
    for flat, slot in ion:
        cond_copies.append(remote(ped, cwin.at[0, slot], cs.at[0, slot], cr.at[0, slot], dev(flat)))
        cond_copies.append(remote(hall, cwin.at[1, slot], cs.at[1, slot], cr.at[1, slot], dev(flat)))
        if slot < 3:
            cond_copies.append(
                remote(shwin.at[1], shwin.at[slot], cs.at[2, slot], cr.at[2, slot], dev(flat)))
    for c in cond_copies:
        c.start()

    for c in local + cond_local:
        c.wait()

    lane = lax.broadcasted_iota(jnp.int32, (cx, cy, nz), 2)
    prim = [win[v, 1:1 + cx, PAD:PAD + cy, :] for v in range(8)]
    terms = cell_terms(prim)
    win[8, 1:1 + cx, PAD:PAD + cy, :] = speed_of(prim, terms, 0)
    each(has_xu, xspeed[0], "start")
    each(has_xd, xspeed[1], "start")
    flux, speed = flux_of(prim, terms, 2), speed_of(prim, terms, 2)
    first, last = lane == 0, lane == nz - 1

    def z_dn(a):
        return jnp.where(first, a, roll(a, 1, 2))

    largest = jnp.maximum(speed, z_dn(speed))
    for v in range(8):
        u, f = terms[0][v], flux[v]
        low = face(None if f is None else z_dn(f), f, z_dn(u), u, largest)
        top = jnp.zeros_like(u) if f is None else f
        high = jnp.where(last, top, roll(low, -1, 2))
        out[v] = u - COURANT * (high - low)

    each(has_yd, yc[0], "wait_recv")
    each(has_yu, yc[1], "wait_recv")

    @pl.when(p == 0)
    def _():
        for v in range(8):
            win[v, 1:1 + cx, PAD - 1:PAD, :] = win[v, 1:1 + cx, PAD:PAD + 1, :]

    @pl.when(p == ny - 1)
    def _():
        for v in range(8):
            win[v, 1:1 + cx, PAD + cy:PAD + cy + 1, :] = win[v, 1:1 + cx, PAD + cy - 1:PAD + cy, :]

    prim = [win[v, 1:1 + cx] for v in range(8)]
    terms = cell_terms(prim)
    flux, speed = flux_of(prim, terms, 1), speed_of(prim, terms, 1)
    largest = jnp.maximum(speed, roll(speed, 1, 1))
    for v in range(8):
        u, f = terms[0][v], flux[v]
        low = face(None if f is None else roll(f, 1, 1), f, roll(u, 1, 1), u, largest)
        diff = roll(low, -1, 1) - low
        out[v] = out[v] - COURANT * diff[:, PAD:PAD + cy, :]

    def edge_planes(which):
        @pl.when(g == 0)
        def _():
            for v in which:
                win[v, 0, PAD:PAD + cy, :] = win[v, 1, PAD:PAD + cy, :]

        @pl.when(g == nx - 1)
        def _():
            for v in which:
                win[v, cx + 1, PAD:PAD + cy, :] = win[v, cx, PAD:PAD + cy, :]

    def planes(v):
        return win[v, :, PAD:PAD + cy, :]

    def x_change(u, f):
        speed = planes(8)
        largest = jnp.maximum(speed[:-1], speed[1:])
        lows = face(None if f is None else f[:-1], None if f is None else f[1:], u[:-1], u[1:], largest)
        return COURANT * (lows[1:] - lows[:-1])

    each(has_xd, xc[0] + xspeed[0], "wait_recv")
    each(has_xu, xc[1] + xspeed[1], "wait_recv")
    edge_planes((1, 2, 3, 4, 5, 6, 8))
    for v in (4, 6, 5):
        u = planes(v)
        f = None if v == 4 else u * planes(1) - planes(4) * planes(v - 3)
        new = out[v] - x_change(u, f)
        out[v] = new
        fwin[{4: 0, 6: 1, 5: 2}[v], 1:1 + cx, PAD:PAD + cy, :] = new
        if v == 5:
            fx = halo_copies([(fwin, 1, 2, (1, PAD, 1))], fwin, fs.at[0], fr.at[0], True)
            fy = halo_copies([(fwin, 0, 2, (1, PAD, 0))], fwin, fs.at[1], fr.at[1], False)
            each(has_xu, fx[0], "start")
            each(has_xd, fx[1], "start")
            each(has_yu, fy[0], "start")
            each(has_yd, fy[1], "start")
            each(has_xu, xlate[0], "start")
            each(has_xd, xlate[1], "start")

    each(has_xd, fx[0], "wait_recv")
    each(has_xu, fx[1], "wait_recv")
    each(has_yd, fy[0], "wait_recv")
    each(has_yu, fy[1], "wait_recv")

    @pl.when(g == 0)
    def _():
        for v in (1, 2):
            fwin[v, 0, PAD:PAD + cy, :] = fwin[v, 1, PAD:PAD + cy, :]

    @pl.when(g == nx - 1)
    def _():
        for v in (1, 2):
            fwin[v, cx + 1, PAD:PAD + cy, :] = fwin[v, cx, PAD:PAD + cy, :]

    @pl.when(p == 0)
    def _():
        for v in (0, 1):
            fwin[v, 1:1 + cx, PAD - 1:PAD, :] = fwin[v, 1:1 + cx, PAD:PAD + 1, :]

    @pl.when(p == ny - 1)
    def _():
        for v in (0, 1):
            fwin[v, 1:1 + cx, PAD + cy:PAD + cy + 1, :] = (
                fwin[v, 1:1 + cx, PAD + cy - 1:PAD + cy, :])

    def d_x(v):
        return 0.5 * (fwin[v, 2:2 + cx, PAD:PAD + cy, :] - fwin[v, 0:cx, PAD:PAD + cy, :])

    def d_y(v):
        a = fwin[v, 1:1 + cx]
        return 0.5 * (roll(a, -1, 1) - roll(a, 1, 1))[:, PAD:PAD + cy, :]

    def d_z(a):
        return 0.5 * (jnp.where(last, a, roll(a, -1, 2)) - z_dn(a))

    bx, bz, by = [fwin[v, 1:1 + cx, PAD:PAD + cy, :] for v in range(3)]
    jx = d_y(1) - d_z(by)
    jy = d_z(bx) - d_x(1)
    jz = d_x(2) - d_y(0)
    size = jnp.sqrt(bx * bx + by * by + bz * bz)
    current = (jx * bx + jy * by + jz * bz) / jnp.maximum(size, 1.0)
    current = current.reshape(cx * cy, nz)

    pairs = nx // 2
    key = owner[0] * ri + line_row[0]
    pair_row = lax.broadcasted_iota(jnp.int32, (2 * ri, cx * cy), 0)
    pair_row = jnp.where(pair_row >= ri, pair_row + (pairs - 1) * ri, pair_row)

    def deposit(q, carry):
        hot = (key == pair_row + q * ri).astype(F32)
        part[q] = jnp.dot(hot, current, precision=lax.Precision.HIGHEST,
                          preferred_element_type=F32).reshape(2, ri, nz)
        return carry

    def send_part(o, at):
        return remote(part.at[o % pairs], part_in.at[at], as_.at[o], ar.at[at], (o, p))

    def send(k, carry):
        send_part((g + k) % nx, g).start()
        return carry

    lax.fori_loop(0, pairs, deposit, 0, unroll=nx <= 8)
    lax.fori_loop(1, nx, send, 0, unroll=nx <= 8)

    for c in cond_copies:
        c.wait_recv()
    wide = 6 * ri
    row = lax.broadcasted_iota(jnp.int32, (wide, nz), 0)
    row = jnp.where(row >= 3 * ri, row - 3 * ri, row)
    place = b % half
    low_row = jnp.where(place == half // 2, ri, 0)
    high_row = jnp.where(place == half // 2 - 1, 2 * ri, 3 * ri)
    valid = (row >= low_row) & (row < high_row)
    pw = jnp.where(valid, cwin[0].reshape(wide, nz), 0.0)
    hw = jnp.where(valid, cwin[1].reshape(wide, nz), 0.0)
    own_shift = shwin[...].reshape(3 * ri, nz)
    col = lax.broadcasted_iota(jnp.int32, (3 * ri, nz), 1)
    cols = jnp.concatenate(
        [(col + own_shift) % nz, (col + (nz - own_shift)) % nz], axis=0)

    def swap(a):
        other = jnp.concatenate([a[3 * ri:], a[:3 * ri]], axis=0)
        return jnp.take_along_axis(other, cols, axis=1)

    def east(a):
        return roll(a, -1, 1)

    def west(a):
        return roll(a, 1, 1)

    def up(a):
        return roll(a, 1, 0)

    def down(a):
        return roll(a, -1, 0)

    he, hwst = east(hw), west(hw)
    coef = [
        0.5 * (pw + up(pw)), 0.5 * (pw + down(pw)),
        0.5 * (pw + east(pw)), 0.5 * (pw + west(pw)),
        0.125 * (hw + up(he)), 0.125 * (hw + up(hwst)),
        0.125 * (hw + down(he)), 0.125 * (hw + down(hwst)),
    ]
    center = coef[0]
    for c in coef[1:]:
        center = center + c
    inv = jnp.where(valid, 1.0 / jnp.where(valid, center, 1.0), 0.0)
    cu, cd, ce, cw, cue, cuw, cde, cdw = [c * inv for c in coef]
    pm = swap(pw)
    both = jnp.where(valid, pw + pm, 1.0)
    wa = jnp.where(valid, pw / both, 0.0)
    wb = jnp.where(valid, pm / both, 0.0)

    each(has_xd, xlate[0], "wait_recv")
    each(has_xu, xlate[1], "wait_recv")
    edge_planes((0, 7))
    prim = [planes(v) for v in range(8)]
    terms = cell_terms(prim)
    flux = flux_of(prim, terms, 0)
    for v in (0, 1, 2, 3, 7):
        out[v] = out[v] - x_change(terms[0][v], flux[v])

    def take_part(k, total):
        s = (g + k) % nx
        send_part(s, s).wait_recv()
        return total + part_in[s]

    total = lax.fori_loop(1, nx, take_part, part[g % pairs], unroll=nx <= 8)
    northern = g < pairs
    swin[0, 1] = jnp.where(northern, total[0], total[1])
    swin[1, 1] = jnp.where(northern, total[1], total[0])
    s_copies = [
        remote(swin.at[:, 1], swin.at[:, slot], ss.at[slot // 2], sr.at[slot // 2], dev(flat))
        for flat, slot in ion[:2]]
    for c in s_copies:
        c.start()
    for c in s_copies:
        c.wait_recv()
    source = swin[...].reshape(wide, nz) * inv

    def couple(phi):
        return wa * phi + wb * swap(phi)

    phi = couple(source)
    for _ in range(SWEEPS - 1):
        e, w = east(phi), west(phi)
        acc = source + ce * e + cw * w
        acc = acc + up_terms(phi, e, w, cu, cue, cuw, up)
        acc = acc + up_terms(phi, e, w, cd, -cde, -cdw, down)
        phi = couple(acc)
    phi_out[...] = phi[ri:2 * ri]

    each(has_xu, xc[0] + xspeed[0] + xlate[0] + fx[0], "wait_send")
    each(has_xd, xc[1] + xspeed[1] + xlate[1] + fx[1], "wait_send")
    each(has_yu, yc[0] + fy[0], "wait_send")
    each(has_yd, yc[1] + fy[1], "wait_send")
    for c in cond_copies + s_copies:
        c.wait_send()

    def sent(k, carry):
        send_part((g + k) % nx, g).wait_send()
        return carry

    lax.fori_loop(1, nx, sent, 0)


def up_terms(phi, e, w, straight, plus, minus, move):
    return straight * move(phi) + plus * move(e) - minus * move(w)


def body(sizes, density, velocity, magnetic, pressure, line_owner, line_row, pedersen, hall, mirror_shift):
    cx, cy, nz = density.shape
    ri = pedersen.shape[0]
    nx = sizes[0]
    any_ = pl.BlockSpec(memory_space=pl.ANY)
    vmem = pl.BlockSpec(memory_space=pltpu.VMEM)
    smem = pl.BlockSpec(memory_space=pltpu.SMEM)
    dma = pltpu.SemaphoreType.DMA
    return pl.pallas_call(
        functools.partial(kernel, sizes),
        out_shape=(
            pltpu.VMEM((8, cx, cy, nz), F32),
            pltpu.VMEM((ri, nz), F32),
        ),
        in_specs=[any_] * 4 + [vmem] * 2 + [any_] * 2 + [smem],
        out_specs=(vmem, vmem),
        scratch_shapes=[
            pltpu.VMEM((9, cx + 2, cy + 2 * PAD, nz), F32),
            pltpu.VMEM((3, cx + 2, cy + 2 * PAD, nz), F32),
            pltpu.VMEM((nx // 2, 2, ri, nz), F32),
            pltpu.VMEM((nx, 2, ri, nz), F32),
            pltpu.VMEM((2, 6, ri, nz), F32),
            pltpu.VMEM((2, 3, ri, nz), F32),
            pltpu.VMEM((3, ri, nz), jnp.int32),
            dma((6,)),
            dma((2, 5)), dma((2, 5)), dma((2, 4)), dma((2, 4)),
            dma((3, 6)), dma((3, 6)),
            dma((2, 2, 1)), dma((2, 2, 1)),
            dma((nx,)), dma((nx,)),
            dma((2,)), dma((2,)),
        ],
        compiler_params=pltpu.CompilerParams(collective_id=0, has_side_effects=True),
        name="flux_and_potential",
    )(density, velocity, magnetic, pressure, line_owner.reshape(1, 1, cx * cy), line_row, pedersen, hall, mirror_shift)


def solution(mesh):
    sizes = (mesh.shape["gx"], mesh.shape["pb"])
    in_specs = (
        P("gx", "pb", None),
        P(None, "gx", "pb", None),
        P(None, "gx", "pb", None),
        P("gx", "pb", None),
        P("gx", "pb", None, None),
        P("gx", "pb", None),
        P(("gx", "pb"), None),
        P(("gx", "pb"), None),
        P(("gx", "pb")),
    )
    out_specs = (P(None, "gx", "pb", None), P(("gx", "pb"), None))
    return jax.shard_map(
        functools.partial(body, sizes), mesh=mesh, in_specs=in_specs, out_specs=out_specs,
        check_vma=False)
```
